128 devices in a mesh: chan: 8 (over y_hi, z), tm: 16 (over x, y_lo, core).
Axes of the slice: x: 4, y: 4 (y_hi: 2, y_lo: 2; y = y_hi * 2 + y_lo), z: 4, core: 2. Of those that a mesh axis runs over, the one named last changes fastest.
Arguments:
- raw_strain: float32 [512, 16384], P('chan', 'tm'), may hold values from -6 to 6
- whitening: float32 [1024], replicated, may hold values from -0.1875 to 0.1875
- block_mask: int32 [8, 8], replicated, may hold values from 0 to 1, as said below
- old_stack: float32 [32, 512, 512], P('tm', 'chan'), may hold values from -6 to 6
Outputs:
- new_stack: float32 [32, 512, 512], P('tm', 'chan')
The draws below stay inside these ranges and needn't reach their ends.
Inputs may be any that keep to these rules, and one draw needn't show every extreme that they name: block_mask[a, b] is 1 exactly where (b - a) mod 8 is below a reach of row a, each reach at least 1, and 0 elsewhere.
All inputs are finite; a program needn't handle non-finite values.
Results may differ from the reference program's by a relative error of at most 0.0018.
Values may be sent and summed in bfloat16 or wider, within the bound.
No kernel may reach another device: no remote copies, remote signals or barrier semaphores. Data moves between devices by JAX's collectives and lax.ppermute only.
A program may use at most 64 MiB of HBM per device.

```python
import jax
import jax.numpy as jnp
from jax import lax

BLOCK = 64
K = 1024
LAGS = 32
CHANNELS = 512
SAMPLES = 16384
NBLK = 8


def draw_block_mask(key, part):
    reaches = jax.random.randint(key, (NBLK,), 1, NBLK + 1)
    counter = jnp.arange(NBLK, dtype=jnp.int32)
    reaches = jnp.where(counter == 0, 1, reaches)
    offsets = (counter[None, :] - counter[:, None]) % NBLK
    return (offsets < reaches[:, None]).astype(jnp.int32)


def steps_of(own_key, shape, split, smallest, top_value):
    gain, own = 1.0, jax.random.fold_in(own_key, 6)
    for dim, shards_of in split:
        draws = jnp.exp(jax.random.uniform(jax.random.fold_in(own, dim), (shards_of,), jnp.float32, smallest / len(split), top_value / len(split)))
        gain = gain * jnp.repeat(draws, shape[dim] // shards_of).reshape([-1 if axis == dim else 1 for axis in range(len(shape))])
    return gain


def scatter_about(rng, dims, width, bound, shards=(), kind=jnp.bfloat16):
    gain = steps_of(rng, dims, shards, -0.22, 0.18) if shards else 1.0
    result = jax.random.normal(rng, dims, jnp.float32) * width * gain
    return jnp.minimum(jnp.maximum(result, -bound), bound).astype(kind)


def setup_inputs(seed: int = 0) -> dict:
    splits = jax.random.split(jax.random.key(seed), 5)
    return {
        "raw_strain": scatter_about(splits[0], (CHANNELS, SAMPLES), 1.0, 6.0, ((0, 8), (1, 16)), jnp.float32),
        "whitening": scatter_about(splits[1], (K,), K ** -0.5, 0.1875, (), jnp.float32),
        "block_mask": draw_block_mask(jax.random.fold_in(splits[4], 71), 0),
        "old_stack": scatter_about(splits[3], (LAGS, CHANNELS, CHANNELS), 1.0, 6.0, ((0, 16), (1, 8)), jnp.float32),
    }


def reference(raw_strain, whitening, block_mask, old_stack):
    samples = raw_strain.shape[1]
    fft_len = samples + 2 * K
    padded = jnp.pad(raw_strain, ((0, 0), (K // 2, K // 2)))
    spectrum = jnp.conj(jnp.fft.rfft(whitening, fft_len)) * jnp.fft.rfft(padded, fft_len, axis=1)
    filtered = jnp.fft.irfft(spectrum, fft_len, axis=1)[:, :samples].astype(jnp.bfloat16)
    wide_data = filtered.astype(jnp.float32)
    extended = jnp.pad(wide_data, ((0, 0), (0, LAGS)))

    def one_lag(offset):
        shifted = lax.dynamic_slice_in_dim(extended, offset, samples, 1)
        return jnp.dot(wide_data, shifted.T, preferred_element_type=jnp.float32)

    lagged = lax.map(one_lag, jnp.arange(LAGS, dtype=jnp.int32))
    weights = jnp.repeat(jnp.repeat(block_mask, BLOCK, axis=0), BLOCK, axis=1).astype(jnp.float32)
    scaling = float(samples) ** -0.5
    return old_stack + (lagged * weights[None, :, :]) * scaling
```

```python
import functools

import jax
import jax.numpy as jnp
from jax import lax
from jax.experimental import pallas as pl
from jax.experimental.pallas import tpu as pltpu
from jax.sharding import Mesh, PartitionSpec as P

CHAN = ("yh", "z")
TIME = ("x", "yl", "c")
VMEM = pl.BlockSpec(memory_space=pltpu.VMEM)
SMEM = pl.BlockSpec(memory_space=pltpu.SMEM)
NT = (((1,), (1,)), ((), ()))
TILE = 256
PAD = 128


def split(value):
    high = value.astype(jnp.bfloat16)
    return high, (value - high.astype(jnp.float32)).astype(jnp.bfloat16)


def taps_kernel(taps_ref, high_ref, low_ref):
    rows, width = high_ref.shape
    taps = taps_ref[...]
    row = jnp.concatenate([taps, jnp.zeros((1, width - taps.shape[1]), jnp.float32)], axis=1)
    matrix = pltpu.roll(jnp.broadcast_to(row, (rows, width)), 0, 1, stride=1, stride_axis=0)
    high_ref[...], low_ref[...] = split(matrix)


def taps_matrix(whitening):
    width = whitening.shape[0] + TILE
    shape = jax.ShapeDtypeStruct((TILE, width), jnp.bfloat16)
    return pl.pallas_call(
        taps_kernel, out_shape=(shape, shape), in_specs=[VMEM], out_specs=(VMEM, VMEM), name="taps"
    )(whitening[None, :])


def filter_kernel(first_ref, low_ref, own_ref, high_ref, mat_high_ref, mat_low_ref, out_ref):
    channels, seg_len = own_ref.shape
    width = mat_high_ref.shape[1]
    blocks = seg_len // TILE + 1
    lead = (blocks * TILE + width - TILE) - (low_ref.shape[1] + seg_len + high_ref.shape[1])
    padded = jnp.concatenate(
        [jnp.zeros((channels, lead), jnp.float32), low_ref[...], own_ref[...], high_ref[...]], axis=1
    )
    x_high, x_low = split(padded)

    def stacked(value):
        return jnp.concatenate(
            [value[:, b * TILE : b * TILE + width] for b in range(blocks)], axis=0
        )

    x_high, x_low = stacked(x_high), stacked(x_low)
    dot = functools.partial(lax.dot_general, dimension_numbers=NT, preferred_element_type=jnp.float32)
    total = dot(x_low, mat_high_ref[...]) + dot(x_high, mat_low_ref[...])
    total = total + dot(x_high, mat_high_ref[...])
    result = jnp.concatenate(
        [total[b * channels : (b + 1) * channels] for b in range(blocks)], axis=1
    )
    before = result[:, TILE - PAD : TILE]
    before = jnp.where(first_ref[0] > 0, jnp.zeros_like(before), before)
    out_ref[:, :PAD] = before.astype(jnp.bfloat16)
    out_ref[:, PAD:] = result[:, TILE:].astype(jnp.bfloat16)


def filter_segment(first, low, own, high, matrices):
    channels, seg_len = own.shape
    return pl.pallas_call(
        filter_kernel,
        out_shape=jax.ShapeDtypeStruct((channels, PAD + seg_len), jnp.bfloat16),
        in_specs=[SMEM] + [VMEM] * 5,
        out_specs=VMEM,
        name="filter",
    )(first, low, own, high, *matrices)


def correlate_kernel(lag_count, place_ref, *refs):
    *piece_refs, mine_ref, theirs_ref, out_ref, rows_ref, cols_ref = refs
    core = place_ref[0]
    half = len(piece_refs) // 2
    channels, seg_len = piece_refs[0].shape
    for index in range(half):
        at = pl.ds(pl.multiple_of(place_ref[1 + index] * channels, channels), channels)
        for side in range(2):
            begin = pl.multiple_of((core if side == 0 else 1 - core) * seg_len, seg_len)
            cols_ref[at, pl.ds(begin, seg_len)] = piece_refs[2 * index + side][...]
    mine, theirs = mine_ref[...], theirs_ref[...]
    first = jnp.where(core == 0, mine, theirs)
    second = jnp.where(core == 0, theirs, mine)
    both = jnp.concatenate([first, second[:, PAD:]], axis=1)
    both = jnp.where(core == 0, both, pltpu.roll(both, 2, 1))
    for index in range(lag_count):
        lag = 4 * (index // 2) + index % 2
        moved = both if lag == 0 else pltpu.roll(both, lag, 1)
        rows_ref[index * channels : (index + 1) * channels, :] = moved[:, PAD:]
    step = 4 * channels
    out_rows = out_ref.shape[0]

    @pl.loop(0, out_rows // step)
    def _(index):
        at = pl.ds(pl.multiple_of(index * step, step), step)
        out_ref[at, :] = lax.dot_general(
            rows_ref[at, :], cols_ref[...], NT, preferred_element_type=jnp.float32
        ).astype(jnp.bfloat16)


def correlate(place, pieces, mine, theirs, lag_count):
    channels, seg_len = pieces[0].shape
    width = channels * (len(pieces) // 2)
    return pl.pallas_call(
        functools.partial(correlate_kernel, lag_count),
        out_shape=jax.ShapeDtypeStruct((lag_count * channels, width), jnp.bfloat16),
        in_specs=[SMEM] + [VMEM] * (len(pieces) + 2),
        out_specs=VMEM,
        scratch_shapes=[
            pltpu.VMEM((lag_count * channels, 2 * seg_len), jnp.bfloat16),
            pltpu.VMEM((width, 2 * seg_len), jnp.bfloat16),
        ],
        name="correlate",
    )(place, *pieces, mine, theirs)


def turned(value, axis, distance):
    size = lax.axis_size(axis)
    return lax.ppermute(value, axis, [(i, (i + distance) % size) for i in range(size)])


def shards(raw_strain, whitening, block_mask, old_stack):
    channels, seg_len = raw_strain.shape
    half_taps = whitening.shape[0] // 2
    segments = lax.axis_size(TIME)
    lag_total = old_stack.shape[0] * segments
    core, z, yh = (lax.axis_index(a) for a in ("c", "z", "yh"))
    segment = lax.axis_index(TIME)
    up = [(i, i + 1) for i in range(segments - 1)]
    low = lax.ppermute(raw_strain[:, seg_len - half_taps - PAD :], TIME, up)
    high = lax.ppermute(raw_strain[:, :half_taps], TIME, [(b, a) for a, b in up])
    matrices = taps_matrix(whitening)
    first = (segment == 0).astype(jnp.int32)[None]
    mine = filter_segment(first, low, raw_strain, high, matrices)
    theirs = turned(mine, "c", 1)
    own = mine[:, PAD:]
    across = turned(own, "yh", 1)
    near = [own] + [turned(own, "z", d) for d in (1, 3, 2)]
    far = [across] + [turned(across, "z", d) for d in (1, 3, 2)]
    pieces = []
    for piece in near + far:
        pieces += [piece, theirs[:, PAD:] if piece is own else turned(piece, "c", 1)]
    zs = lax.axis_size("z")
    turns = [(z - d) % zs for d in (0, 1, 3, 2)]
    places = [yh * zs + t for t in turns] + [(1 - yh) * zs + t for t in turns]
    place = jnp.stack([core] + places).astype(jnp.int32)
    partial = correlate(place, pieces, mine, theirs, lag_total // 2)
    groups = segments // 2
    partial = partial.reshape(groups, lag_total // segments, channels, -1)
    received = lax.all_to_all(partial, ("x", "yl"), 0, 0)
    summed = jnp.sum(received.astype(jnp.float32), axis=0)
    scaling = float(seg_len * segments) ** (-0.5)
    weights = jnp.repeat(block_mask[yh * zs + z].astype(jnp.float32) * scaling, channels)
    return old_stack + summed * weights[None, None, :]


def solution(mesh):
    fine = Mesh(mesh.devices.reshape(2, 4, 4, 2, 2), CHAN + TIME)
    in_specs = (P(CHAN, TIME), P(), P(), P(TIME, CHAN, None))
    out_specs = P(TIME, CHAN, None)
    return jax.shard_map(shards, mesh=fine, in_specs=in_specs, out_specs=out_specs, check_vma=False)
```

```python
import functools

import jax
import jax.numpy as jnp
from jax import lax
from jax.experimental import pallas as pl
from jax.experimental.pallas import tpu as pltpu
from jax.sharding import Mesh, PartitionSpec as P


CHAN = ("yh", "z")
TIME = ("x", "yl", "c")
OWNERS = ("yh", "x", "yl")
VMEM = pl.BlockSpec(memory_space=pltpu.VMEM)
SMEM = pl.BlockSpec(memory_space=pltpu.SMEM)
NT = (((1,), (1,)), ((), ()))
TILE = 256
PAD = 128
MIB = 1 << 20


def call(kernel, out_shape, operands, mib, flops, specs=None):
    return pl.pallas_call(
        kernel,
        out_shape=out_shape,
        in_specs=specs or [VMEM] * len(operands),
        out_specs=jax.tree.map(lambda _: VMEM, out_shape),
        compiler_params=pltpu.CompilerParams(vmem_limit_bytes=mib * MIB),
        cost_estimate=pl.CostEstimate(flops=flops, bytes_accessed=MIB, transcendentals=0),
    )(*operands)


def split(value):
    high = value.astype(jnp.bfloat16)
    return high, (value - high.astype(jnp.float32)).astype(jnp.bfloat16)


def prepare_kernel(taps_ref, own_ref, high_ref, low_ref, own_high_ref, own_low_ref):
    own_high_ref[...], own_low_ref[...] = split(own_ref[...])
    rows, width = high_ref.shape
    taps = taps_ref[...]
    row = jnp.concatenate([taps, jnp.zeros((1, width - taps.shape[1]), jnp.float32)], axis=1)
    matrix = pltpu.roll(jnp.broadcast_to(row, (rows, width)), 0, 1, stride=1, stride_axis=0)
    high_ref[...], low_ref[...] = split(matrix)


def prepare(whitening, own):
    matrix = jax.ShapeDtypeStruct((TILE, whitening.shape[0] + TILE), jnp.bfloat16)
    part = jax.ShapeDtypeStruct(own.shape, jnp.bfloat16)
    shapes = (matrix, matrix, part, part)
    return call(prepare_kernel, shapes, (whitening[None, :], own), 8, 10**9)


def filter_kernel(
    half_taps, place_ref, beside_ref, across_ref, mat_high_ref, mat_low_ref, own_high_ref, own_low_ref, mine_ref, own_ref
):
    channels, seg_len = own_ref.shape
    width = mat_high_ref.shape[1]
    blocks = seg_len // TILE + 1
    lower = place_ref[0] == 0
    reach = half_taps + PAD
    across = across_ref[...]
    low = split(jnp.where(lower, across, beside_ref[:, seg_len - reach :]))
    high = split(jnp.where(lower, beside_ref[:, :half_taps], across[:, :half_taps]))

    def stacked(before, own, after):
        zeros = jnp.zeros((channels, TILE - PAD), jnp.bfloat16)
        padded = jnp.concatenate([zeros, before, own, after], axis=1)
        return jnp.concatenate(
            [padded[:, b * TILE : b * TILE + width] for b in range(blocks)], axis=0
        )

    x_high = stacked(low[0], own_high_ref[...], high[0])
    x_low = stacked(low[1], own_low_ref[...], high[1])
    dot = functools.partial(lax.dot_general, dimension_numbers=NT, preferred_element_type=jnp.float32)
    total = dot(x_low, mat_high_ref[...]) + dot(x_high, mat_low_ref[...])
    total = total + dot(x_high, mat_high_ref[...])
    before = total[:channels, TILE - PAD :]
    before = jnp.where(place_ref[1] == 0, jnp.zeros_like(before), before)
    mine_ref[:, :PAD] = before.astype(jnp.bfloat16)
    for b in range(1, blocks):
        piece = total[b * channels : (b + 1) * channels].astype(jnp.bfloat16)
        mine_ref[:, PAD + (b - 1) * TILE : PAD + b * TILE] = piece
        own_ref[:, (b - 1) * TILE : b * TILE] = piece


def filter_segment(place, beside, across, prepared, half_taps):
    channels, seg_len = beside.shape
    return call(
        functools.partial(filter_kernel, half_taps),
        (
            jax.ShapeDtypeStruct((channels, PAD + seg_len), jnp.bfloat16),
            jax.ShapeDtypeStruct((channels, seg_len), jnp.bfloat16),
        ),
        (place, beside, across, *prepared),
        12,
        10**9,
        [SMEM] + [VMEM] * 6,
    )


def rows_kernel(lag_count, place_ref, mine_ref, theirs_ref, rows_ref):
    channels = mine_ref.shape[0]
    core = place_ref[0]
    mine, theirs = mine_ref[...], theirs_ref[...]
    first = jnp.where(core == 0, mine, theirs)
    second = jnp.where(core == 0, theirs, mine)
    both = jnp.concatenate([first, second[:, PAD:]], axis=1)
    both = jnp.where(core == 0, both, pltpu.roll(both, 2, 1))
    for index in range(lag_count):
        lag = 4 * (index // 2) + index % 2
        moved = both if lag == 0 else pltpu.roll(both, lag, 1)
        rows_ref[index * channels : (index + 1) * channels, :] = moved[:, PAD:]


def lagged_rows(place, mine, theirs, lag_count):
    channels, width = mine.shape
    return call(
        functools.partial(rows_kernel, lag_count),
        jax.ShapeDtypeStruct((lag_count * channels, 2 * (width - PAD)), jnp.bfloat16),
        (place, mine, theirs),
        8,
        2 * 10**9,
        [SMEM, VMEM, VMEM],
    )


def correlate_kernel(place_ref, *refs):
    *piece_refs, mine_ref, other_ref, out_ref, cols_ref = refs
    core, yh = place_ref[0], place_ref[2]
    half = len(piece_refs) // 2
    channels, seg_len = piece_refs[0].shape
    side = pl.program_id(0)

    @pl.when(side == 0)
    def _():
        for index in range(half):
            at = pl.ds(pl.multiple_of(place_ref[3 + index] * channels, channels), channels)
            for k in range(2):
                begin = pl.multiple_of((core if k == 0 else 1 - core) * seg_len, seg_len)
                cols_ref[at, pl.ds(begin, seg_len)] = piece_refs[2 * index + k][...]

    def fill(rows_ref):
        out_ref[0] = lax.dot_general(
            rows_ref[...], cols_ref[...], NT, preferred_element_type=jnp.float32
        ).astype(jnp.bfloat16)

    pl.when(side == yh)(lambda: fill(mine_ref))
    pl.when(side != yh)(lambda: fill(other_ref))


def correlate(place, pieces, mine_rows, other_rows):
    channels, seg_len = pieces[0].shape
    width = channels * (len(pieces) // 2)
    rows = mine_rows.shape[0]
    return pl.pallas_call(
        correlate_kernel,
        grid=(2,),
        out_shape=jax.ShapeDtypeStruct((2, rows, width), jnp.bfloat16),
        in_specs=[SMEM] + [VMEM] * (len(pieces) + 2),
        out_specs=pl.BlockSpec((1, rows, width), lambda side: (side, 0, 0)),
        scratch_shapes=[pltpu.VMEM((width, 2 * seg_len), jnp.bfloat16)],
        compiler_params=pltpu.CompilerParams(vmem_limit_bytes=20 * MIB),
        cost_estimate=pl.CostEstimate(flops=4 * 10**9, bytes_accessed=MIB, transcendentals=0),
        name="correlate",
    )(place, *pieces, mine_rows, other_rows)


def stack_kernel(parts_ref, weights_ref, old_ref, out_ref):
    width = parts_ref.shape[-1]
    count = parts_ref.shape[1]
    for side in range(2):
        at = slice(side * width, (side + 1) * width)
        total = parts_ref[side, 0].astype(jnp.float32)
        for k in range(1, count):
            total = total + parts_ref[side, k].astype(jnp.float32)
        out_ref[:, at] = old_ref[:, at] + total * weights_ref[:, at]


def stack(parts, weights, old_stack):
    lags, channels, width = old_stack.shape
    parts = parts.reshape(2, -1, lags * channels, parts.shape[-1])
    shape = jax.ShapeDtypeStruct((lags * channels, width), jnp.float32)
    old = old_stack.reshape(lags * channels, width)
    return call(stack_kernel, shape, (parts, weights, old), 8, 10**8).reshape(old_stack.shape)


def turned(value, axis, distance):
    size = lax.axis_size(axis)
    return lax.ppermute(value, axis, [(i, (i + distance) % size) for i in range(size)])


def shards(raw_strain, whitening, block_mask, old_stack):
    channels, seg_len = raw_strain.shape
    half_taps = whitening.shape[0] // 2
    segments = lax.axis_size(TIME)
    lags = old_stack.shape[0]
    core, z, yh, zs = lax.axis_index("c"), lax.axis_index("z"), lax.axis_index("yh"), lax.axis_size("z")
    distances = (0, 2, 1, 3)
    place = [core, lax.axis_index(TIME), yh] + [(z - d) % zs for d in distances]
    place = jnp.stack(place).astype(jnp.int32)
    reach = half_taps + PAD
    edge = jnp.where(core == 0, raw_strain[:, :reach], raw_strain[:, seg_len - reach :])
    pairs = [(i, i + 1) for i in range(1, segments - 1, 2)]
    across = lax.ppermute(edge, TIME, pairs + [(b, a) for a, b in pairs])
    beside = turned(raw_strain, "c", 1)
    prepared = prepare(whitening, raw_strain)
    mine, own = filter_segment(place, beside, across, prepared, half_taps)
    other = turned(mine, "yh", 1)
    pieces = []
    for d in distances:
        piece = turned(own, "z", d) if d else own
        pieces += [piece, turned(piece, "c", 1)]
    lag_count = lags * segments // 2
    mine_swapped = turned(mine, "c", 1)
    other_swapped = turned(other, "c", 1)
    mine_rows = lagged_rows(place, mine, mine_swapped, lag_count)
    other_rows = lagged_rows(place, other, other_swapped, lag_count)
    partial = correlate(place, pieces, mine_rows, other_rows)
    partial = partial.reshape(segments, lags, channels, -1)
    received = lax.all_to_all(partial, OWNERS, 0, 0)
    scaling = float(seg_len * segments) ** (-0.5)
    weights = jnp.repeat(block_mask[yh * zs + z].astype(jnp.float32) * scaling, channels)[None, :]
    return stack(received, weights, old_stack)


def solution(mesh):
    fine = Mesh(mesh.devices.reshape(2, 4, 4, 2, 2), CHAN + TIME)
    in_specs = (P(CHAN, TIME), P(), P(), P(TIME, CHAN, None))
    out_specs = P(TIME, CHAN, None)
    return jax.shard_map(shards, mesh=fine, in_specs=in_specs, out_specs=out_specs, check_vma=False)
```

```python
import functools

import jax
import jax.numpy as jnp
from jax import lax
from jax.experimental import pallas as pl
from jax.experimental.pallas import tpu as pltpu
from jax.sharding import Mesh, PartitionSpec as P


CHAN = ("yh", "z")
TIME = ("x", "yl", "c")
OWNERS = ("yh", "x", "yl")
VMEM = pl.BlockSpec(memory_space=pltpu.VMEM)
NT = (((1,), (1,)), ((), ()))
TILE = 256
PAD = 128
MIB = 1 << 20


def call(kernel, out_shape, operands, mib, flops):
    return pl.pallas_call(
        kernel,
        out_shape=out_shape,
        in_specs=[VMEM] * len(operands),
        out_specs=jax.tree.map(lambda _: VMEM, out_shape),
        compiler_params=pltpu.CompilerParams(vmem_limit_bytes=mib * MIB),
        cost_estimate=pl.CostEstimate(flops=flops, bytes_accessed=MIB, transcendentals=0),
    )(*operands)


def edge_kernel(own_ref, edge_ref):
    width = edge_ref.shape[1]
    lower = lax.axis_index("c") == 0
    pl.when(lower)(lambda: pltpu.sync_copy(own_ref.at[:, :width], edge_ref))
    pl.when(jnp.logical_not(lower))(lambda: pltpu.sync_copy(own_ref.at[:, own_ref.shape[1] - width :], edge_ref))


def facing_edge(own, width):
    return pl.pallas_call(
        edge_kernel,
        out_shape=jax.ShapeDtypeStruct((own.shape[0], width), own.dtype),
        in_specs=[pl.BlockSpec(memory_space=pl.ANY)],
        out_specs=VMEM,
        compiler_params=pltpu.CompilerParams(vmem_limit_bytes=2 * MIB),
        name="edge",
    )(own)


def split(value):
    high = value.astype(jnp.bfloat16)
    return high, (value - high.astype(jnp.float32)).astype(jnp.bfloat16)


def prepare_kernel(taps_ref, own_ref, high_ref, low_ref, own_high_ref, own_low_ref):
    own_high_ref[...], own_low_ref[...] = split(own_ref[...])
    rows, width = high_ref.shape
    taps = taps_ref[...]
    row = jnp.concatenate([taps, jnp.zeros((1, width - taps.shape[1]), jnp.float32)], axis=1)
    matrix = pltpu.roll(jnp.broadcast_to(row, (rows, width)), 0, 1, stride=1, stride_axis=0)
    high_ref[...], low_ref[...] = split(matrix)


def prepare(whitening, own):
    matrix = jax.ShapeDtypeStruct((TILE, whitening.shape[0] + TILE), jnp.bfloat16)
    part = jax.ShapeDtypeStruct(own.shape, jnp.bfloat16)
    shapes = (matrix, matrix, part, part)
    return call(prepare_kernel, shapes, (whitening[None, :], own), 8, 10**9)


def filter_kernel(
    half_taps, beside_ref, across_ref, mat_high_ref, mat_low_ref, own_high_ref, own_low_ref, mine_ref, own_ref
):
    channels, seg_len = own_ref.shape
    width = mat_high_ref.shape[1]
    blocks = seg_len // TILE + 1
    lower = lax.axis_index("c") == 0
    reach = half_taps + PAD
    across = across_ref[...]
    low = split(jnp.where(lower, across, beside_ref[:, seg_len - reach :]))
    high = split(jnp.where(lower, beside_ref[:, :half_taps], across[:, :half_taps]))

    def stacked(before, own, after):
        zeros = jnp.zeros((channels, TILE - PAD), jnp.bfloat16)
        padded = jnp.concatenate([zeros, before, own, after], axis=1)
        return jnp.concatenate(
            [padded[:, b * TILE : b * TILE + width] for b in range(blocks)], axis=0
        )

    x_high = stacked(low[0], own_high_ref[...], high[0])
    x_low = stacked(low[1], own_low_ref[...], high[1])
    dot = functools.partial(lax.dot_general, dimension_numbers=NT, preferred_element_type=jnp.float32)
    total = dot(x_low, mat_high_ref[...]) + dot(x_high, mat_low_ref[...])
    total = total + dot(x_high, mat_high_ref[...])
    before = total[:channels, TILE - PAD :]
    before = jnp.where(lax.axis_index(TIME) == 0, jnp.zeros_like(before), before)
    mine_ref[:, :PAD] = before.astype(jnp.bfloat16)
    for b in range(1, blocks):
        piece = total[b * channels : (b + 1) * channels].astype(jnp.bfloat16)
        mine_ref[:, PAD + (b - 1) * TILE : PAD + b * TILE] = piece
        own_ref[:, (b - 1) * TILE : b * TILE] = piece


def filter_segment(beside, across, prepared, half_taps):
    channels, seg_len = beside.shape
    return call(
        functools.partial(filter_kernel, half_taps),
        (
            jax.ShapeDtypeStruct((channels, PAD + seg_len), jnp.bfloat16),
            jax.ShapeDtypeStruct((channels, seg_len), jnp.bfloat16),
        ),
        (beside, across, *prepared),
        12,
        10**9,
    )


def rows_kernel(lag_count, mine_ref, theirs_ref, rows_ref):
    channels, seg_len = mine_ref.shape[0], mine_ref.shape[1] - PAD
    core = lax.axis_index("c")
    mine, theirs = mine_ref[...], theirs_ref[...]
    first = jnp.where(core == 0, mine, theirs)
    second = jnp.where(core == 0, theirs, mine)
    both = jnp.concatenate([first, second[:, PAD:]], axis=1)
    both = jnp.where(core == 0, both, pltpu.roll(both, 2, 1))
    for index in range(lag_count):
        lag = 4 * (index // 2) + index % 2
        moved = both if lag == 0 else pltpu.roll(both, lag, 1)
        at = slice(index * channels, (index + 1) * channels)
        for k in range(2):
            begin = pl.multiple_of((core if k == 0 else 1 - core) * seg_len, seg_len)
            rows_ref[at, pl.ds(begin, seg_len)] = moved[:, PAD + k * seg_len : PAD + (k + 1) * seg_len]


def lagged_rows(mine, theirs, lag_count):
    channels, width = mine.shape
    return call(
        functools.partial(rows_kernel, lag_count),
        jax.ShapeDtypeStruct((lag_count * channels, 2 * (width - PAD)), jnp.bfloat16),
        (mine, theirs),
        8,
        2 * 10**9,
    )


def correlate_kernel(*refs):
    *piece_refs, mine_ref, other_ref, out_ref = refs
    split_at = len(piece_refs) - 2
    seg_len = piece_refs[0].shape[1]
    side = pl.program_id(0)

    def fill(rows_ref):
        total = 0.0
        for k in range(2):
            refs = piece_refs[split_at:] if k else piece_refs[:split_at]
            cols = jnp.concatenate([ref[:, ref.shape[1] - seg_len :] for ref in refs], axis=0)
            rows = rows_ref[:, k * seg_len : (k + 1) * seg_len]
            total = total + lax.dot_general(rows, cols, NT, preferred_element_type=jnp.float32)
        out_ref[0] = total.astype(jnp.bfloat16)

    pl.when(side == lax.axis_index("yh"))(lambda: fill(mine_ref))
    pl.when(side != lax.axis_index("yh"))(lambda: fill(other_ref))


def correlate(pieces, mine_rows, other_rows):
    width = pieces[0].shape[0] * (len(pieces) - 2)
    rows = mine_rows.shape[0]
    return pl.pallas_call(
        correlate_kernel,
        grid=(2,),
        out_shape=jax.ShapeDtypeStruct((2, rows, width), jnp.bfloat16),
        in_specs=[VMEM] * (len(pieces) + 2),
        out_specs=pl.BlockSpec((1, rows, width), lambda side: (side, 0, 0)),
        compiler_params=pltpu.CompilerParams(vmem_limit_bytes=6 * MIB),
        cost_estimate=pl.CostEstimate(flops=4 * 10**9, bytes_accessed=MIB, transcendentals=0),
        name="correlate",
    )(*pieces, mine_rows, other_rows)


def stack_kernel(parts_ref, weights_ref, old_ref, out_ref):
    count, width = parts_ref.shape[1], parts_ref.shape[-1]
    for side in range(2):
        at = slice(side * width, (side + 1) * width)
        total = parts_ref[side, 0].astype(jnp.float32)
        for k in range(1, count):
            total = total + parts_ref[side, k].astype(jnp.float32)
        total = pltpu.roll(total, lax.axis_index("z") * parts_ref.shape[2] // 2, 1)
        out_ref[:, at] = old_ref[:, at] + total * weights_ref[:, at]


def stack(parts, weights, old_stack):
    lags, channels, width = old_stack.shape
    parts = parts.reshape(2, -1, lags * channels, parts.shape[-1])
    shape = jax.ShapeDtypeStruct((lags * channels, width), jnp.float32)
    old = old_stack.reshape(lags * channels, width)
    return call(stack_kernel, shape, (parts, weights, old), 8, 10**8).reshape(old_stack.shape)


def turned(value, axis, distance):
    size = lax.axis_size(axis)
    return lax.ppermute(value, axis, [(i, (i + distance) % size) for i in range(size)])


def shards(raw_strain, whitening, block_mask, old_stack):
    channels, seg_len = raw_strain.shape
    half_taps = whitening.shape[0] // 2
    segments = lax.axis_size(TIME)
    lags = old_stack.shape[0]
    z, yh, zs = lax.axis_index("z"), lax.axis_index("yh"), lax.axis_size("z")
    reach = half_taps + PAD
    edge = facing_edge(raw_strain, reach)
    pairs = [(i, i + 1) for i in range(1, segments - 1, 2)]
    across = lax.ppermute(edge, TIME, pairs + [(b, a) for a, b in pairs])
    beside = turned(raw_strain, "c", 1)
    prepared = prepare(whitening, raw_strain)
    mine, own = filter_segment(beside, across, prepared, half_taps)
    other = turned(mine, "yh", 1)
    pieces = []
    for d in range(zs):
        piece = turned(own, "z", (zs - d) % zs) if d else own
        pieces.append(piece)
    mine_swapped = turned(mine, "c", 1)
    pieces += [mine_swapped, turned(jnp.concatenate(pieces[1:], axis=0), "c", 1)]
    lag_count = lags * segments // 2
    other_swapped = turned(other, "c", 1)
    mine_rows = lagged_rows(mine, mine_swapped, lag_count)
    other_rows = lagged_rows(other, other_swapped, lag_count)
    partial = correlate(pieces, mine_rows, other_rows)
    partial = partial.reshape(segments, lags, channels, -1)
    received = lax.all_to_all(partial, OWNERS, 0, 0)
    scaling = float(seg_len * segments) ** (-0.5)
    weights = jnp.repeat(block_mask[yh * zs + z].astype(jnp.float32) * scaling, channels)[None, :]
    return stack(received, weights, old_stack)


def solution(mesh):
    fine = Mesh(mesh.devices.reshape(2, 4, 4, 2, 2), CHAN + TIME)
    in_specs = (P(CHAN, TIME), P(), P(), P(TIME, CHAN, None))
    out_specs = P(TIME, CHAN, None)
    return jax.shard_map(shards, mesh=fine, in_specs=in_specs, out_specs=out_specs, check_vma=False)
```

```python
import functools

import jax
import jax.numpy as jnp
from jax import lax
from jax.experimental import pallas as pl
from jax.experimental.pallas import tpu as pltpu
from jax.sharding import Mesh, PartitionSpec as P


CHAN = ("yh", "z")
TIME = ("x", "yl", "c")
VMEM = pl.BlockSpec(memory_space=pltpu.VMEM)
NT = (((1,), (1,)), ((), ()))
TILE = 256
PAD = 128
MIB = 1 << 20


def call(kernel, out_shape, operands, mib, flops):
    return pl.pallas_call(
        kernel,
        out_shape=out_shape,
        in_specs=[VMEM] * len(operands),
        out_specs=jax.tree.map(lambda _: VMEM, out_shape),
        compiler_params=pltpu.CompilerParams(vmem_limit_bytes=mib * MIB),
        cost_estimate=pl.CostEstimate(flops=flops, bytes_accessed=MIB, transcendentals=0),
    )(*operands)


def edge_kernel(own_ref, edge_ref):
    width = edge_ref.shape[1]
    lower = lax.axis_index("c") == 0
    pl.when(lower)(lambda: pltpu.sync_copy(own_ref.at[:, :width], edge_ref))
    pl.when(jnp.logical_not(lower))(lambda: pltpu.sync_copy(own_ref.at[:, own_ref.shape[1] - width :], edge_ref))


def facing_edge(own, width):
    return pl.pallas_call(
        edge_kernel,
        out_shape=jax.ShapeDtypeStruct((own.shape[0], width), own.dtype),
        in_specs=[pl.BlockSpec(memory_space=pl.ANY)],
        out_specs=VMEM,
        compiler_params=pltpu.CompilerParams(vmem_limit_bytes=2 * MIB),
        name="edge",
    )(own)


def split(value):
    high = value.astype(jnp.bfloat16)
    return high, (value - high.astype(jnp.float32)).astype(jnp.bfloat16)


def prepare_kernel(taps_ref, own_ref, high_ref, low_ref, own_high_ref, own_low_ref):
    own_high_ref[...], own_low_ref[...] = split(own_ref[...])
    rows, width = high_ref.shape
    taps = taps_ref[...]
    row = jnp.concatenate([taps, jnp.zeros((1, width - taps.shape[1]), jnp.float32)], axis=1)
    matrix = pltpu.roll(jnp.broadcast_to(row, (rows, width)), 0, 1, stride=1, stride_axis=0)
    high_ref[...], low_ref[...] = split(matrix)


def prepare(whitening, own):
    matrix = jax.ShapeDtypeStruct((TILE, whitening.shape[0] + TILE), jnp.bfloat16)
    part = jax.ShapeDtypeStruct(own.shape, jnp.bfloat16)
    shapes = (matrix, matrix, part, part)
    return call(prepare_kernel, shapes, (whitening[None, :], own), 8, 10**9)


def filter_kernel(
    half_taps, beside_ref, across_ref, mat_high_ref, mat_low_ref, own_high_ref, own_low_ref, mine_ref, own_ref
):
    channels, seg_len = own_ref.shape
    width = mat_high_ref.shape[1]
    blocks = seg_len // TILE + 1
    lower = lax.axis_index("c") == 0
    reach = half_taps + PAD
    across = across_ref[...]
    low = split(jnp.where(lower, across, beside_ref[:, seg_len - reach :]))
    high = split(jnp.where(lower, beside_ref[:, :half_taps], across[:, :half_taps]))

    def stacked(before, own, after):
        zeros = jnp.zeros((channels, TILE - PAD), jnp.bfloat16)
        padded = jnp.concatenate([zeros, before, own, after], axis=1)
        return jnp.concatenate(
            [padded[:, b * TILE : b * TILE + width] for b in range(blocks)], axis=0
        )

    x_high = stacked(low[0], own_high_ref[...], high[0])
    x_low = stacked(low[1], own_low_ref[...], high[1])
    dot = functools.partial(lax.dot_general, dimension_numbers=NT, preferred_element_type=jnp.float32)
    total = dot(x_low, mat_high_ref[...]) + dot(x_high, mat_low_ref[...])
    total = total + dot(x_high, mat_high_ref[...])
    before = total[:channels, TILE - PAD :]
    before = jnp.where(lax.axis_index(TIME) == 0, jnp.zeros_like(before), before)
    mine_ref[:, :PAD] = before.astype(jnp.bfloat16)
    for b in range(1, blocks):
        piece = total[b * channels : (b + 1) * channels].astype(jnp.bfloat16)
        mine_ref[:, PAD + (b - 1) * TILE : PAD + b * TILE] = piece
        own_ref[:, (b - 1) * TILE : b * TILE] = piece


def filter_segment(beside, across, prepared, half_taps):
    channels, seg_len = beside.shape
    return call(
        functools.partial(filter_kernel, half_taps),
        (
            jax.ShapeDtypeStruct((channels, PAD + seg_len), jnp.bfloat16),
            jax.ShapeDtypeStruct((channels, seg_len), jnp.bfloat16),
        ),
        (beside, across, *prepared),
        12,
        10**9,
    )


def rows_kernel(lag_count, mine_ref, theirs_ref, rows_ref):
    channels, seg_len = mine_ref.shape[0], mine_ref.shape[1] - PAD
    core = lax.axis_index("c")
    mine, theirs = mine_ref[...], theirs_ref[...]
    first = jnp.where(core == 0, mine, theirs)
    second = jnp.where(core == 0, theirs, mine)
    both = jnp.concatenate([first, second[:, PAD:]], axis=1)
    both = jnp.where(core == 0, both, pltpu.roll(both, 2, 1))
    for index in range(lag_count):
        group, second = index // 2, index % 2
        lag = 4 * group + second
        moved = both if lag == 0 else pltpu.roll(both, lag, 1)
        groups = lag_count // 2
        place = jnp.where(core == 0, group, group % 2 * (groups // 2) + group // 2)
        at = pl.ds(pl.multiple_of((2 * place + second) * channels, channels), channels)
        for k in range(2):
            begin = pl.multiple_of((core if k == 0 else 1 - core) * seg_len, seg_len)
            rows_ref[at, pl.ds(begin, seg_len)] = moved[:, PAD + k * seg_len : PAD + (k + 1) * seg_len]


def lagged_rows(mine, theirs, lag_count):
    channels, width = mine.shape
    return call(
        functools.partial(rows_kernel, lag_count),
        jax.ShapeDtypeStruct((lag_count * channels, 2 * (width - PAD)), jnp.bfloat16),
        (mine, theirs),
        8,
        2 * 10**9,
    )


def position():
    core, x, y = lax.axis_index("c"), lax.axis_index("x"), 2 * lax.axis_index("yh") + lax.axis_index("yl")
    return core, x, y


def chunk_kernel(distance, *refs):
    *piece_refs, mine_ref, other_ref, out_ref = refs
    seg_len = piece_refs[0].shape[1]
    rows = out_ref.shape[0] // 2
    core, x, y = position()
    yh = lax.axis_index("yh")
    to_x, to_y = lax.rem(x + distance, 4), lax.rem(y + distance, 4)

    def fill(first_ref, second_ref, first_at, second_at):
        total = 0.0
        for k in range(2):
            refs = piece_refs[-2:] if k else piece_refs[:-2]
            cols = jnp.concatenate([ref[:, ref.shape[1] - seg_len :] for ref in refs], axis=0)
            part = slice(k * seg_len, (k + 1) * seg_len)
            left = jnp.concatenate(
                [
                    ref[pl.ds(pl.multiple_of(at, rows), rows), part]
                    for ref, at in ((first_ref, first_at), (second_ref, second_at))
                ],
                axis=0,
            )
            total = total + lax.dot_general(left, cols, NT, preferred_element_type=jnp.float32)
        out_ref[...] = total.astype(out_ref.dtype)

    along_x = to_x * rows
    along_y = lax.rem(to_y, 2) * 2 * rows
    stays = to_y // 2 == yh
    is_x = core == 0

    @pl.when(is_x & (yh == 0))
    def _():
        fill(mine_ref, other_ref, along_x, along_x)

    @pl.when(is_x & (yh != 0))
    def _():
        fill(other_ref, mine_ref, along_x, along_x)

    @pl.when(jnp.logical_not(is_x) & stays)
    def _():
        fill(mine_ref, mine_ref, along_y, along_y + rows)

    @pl.when(jnp.logical_not(is_x) & jnp.logical_not(stays))
    def _():
        fill(other_ref, other_ref, along_y, along_y + rows)


def chunk(pieces, mine_rows, other_rows, distance):
    width = pieces[0].shape[0] * (len(pieces) - 2)
    kind = jnp.bfloat16 if distance else jnp.float32
    return call(
        functools.partial(chunk_kernel, distance),
        jax.ShapeDtypeStruct((mine_rows.shape[0] // 2, width), kind),
        (*pieces, mine_rows, other_rows),
        6,
        10**9,
    )


def by_column_half(own, first, second, third):
    last = lax.axis_index("yl") == 0
    near, far = jnp.where(last, third, first), jnp.where(last, first, third)
    return own + near, second + far


def middle_kernel(own_ref, first_ref, second_ref, third_ref, own_out_ref, *out_refs):
    rows = own_out_ref.shape[1]
    core, x, y = position()
    base = jnp.where(core == 0, y, x)
    for distance, out_ref in enumerate((own_out_ref, *out_refs)):
        at = pl.ds(pl.multiple_of(lax.rem(base + distance, 4) * rows, rows), rows)
        own = own_ref[at, :]
        parts = [ref[at, :].astype(jnp.float32) for ref in (first_ref, second_ref, third_ref)]
        total = own + parts[0] + parts[1] + parts[2]
        same, cross = by_column_half(own, *parts)
        if distance == 0:
            out_ref[0] = jnp.where(core == 0, total, same)
            out_ref[1] = jnp.where(core == 0, jnp.zeros_like(total), cross)
        else:
            rounded = total.astype(jnp.bfloat16).astype(jnp.float32)
            out_ref[0] = jnp.where(core == 0, rounded, same).astype(jnp.bfloat16)
            out_ref[1] = jnp.where(core == 0, total - rounded, cross).astype(jnp.bfloat16)


def middle(own, first, second, third):
    rows, width = own.shape
    shape = (2, rows // 4, width)
    shapes = (jax.ShapeDtypeStruct(shape, jnp.float32),) + (jax.ShapeDtypeStruct(shape, jnp.bfloat16),) * 3
    return call(middle_kernel, shapes, (own, first, second, third), 8, 10**9)


def stack_kernel(own_ref, first_ref, second_ref, third_ref, weights_ref, old_ref, out_ref):
    width = own_ref.shape[-1]
    core, _, _ = position()
    yh = lax.axis_index("yh")
    pairs = [[ref[h].astype(jnp.float32) for h in range(2)] for ref in (first_ref, second_ref, third_ref)]
    x_last = [own_ref[h] + pairs[0][h] + pairs[1][h] + pairs[2][h] for h in range(2)]
    y_last = by_column_half(own_ref[0], *[a + b for a, b in pairs])
    turn = lax.axis_index("z") * (out_ref.shape[0] // 2)
    for h in range(2):
        total = pltpu.roll(jnp.where(core == 0, y_last[h], x_last[h]), turn, 1)
        half = yh if h == 0 else 1 - yh
        at = pl.ds(pl.multiple_of(half * width, width), width)
        out_ref[:, at] = old_ref[:, at] + total * weights_ref[:, at]


def stack(parts, weights, old_stack):
    lags, channels, width = old_stack.shape
    shape = jax.ShapeDtypeStruct((lags * channels, width), jnp.float32)
    old = old_stack.reshape(lags * channels, width)
    return call(stack_kernel, shape, (*parts, weights, old), 8, 10**8).reshape(old_stack.shape)


def passed(value, distance, x_core):
    axes = ("yh", "x", "yl", "c")
    pairs = []
    for x in range(4):
        for y in range(4):
            for core in range(2):
                to_x, to_y = ((x + distance) % 4, y) if core == x_core else (x, (y + distance) % 4)
                source, target = (((b // 2 * 4 + a) * 2 + b % 2) * 2 + core for a, b in ((x, y), (to_x, to_y)))
                pairs.append((source, target))
    return lax.ppermute(value, axes, pairs)


def turned(value, axis, distance):
    size = lax.axis_size(axis)
    return lax.ppermute(value, axis, [(i, (i + distance) % size) for i in range(size)])


def shards(raw_strain, whitening, block_mask, old_stack):
    channels, seg_len = raw_strain.shape
    half_taps = whitening.shape[0] // 2
    segments = lax.axis_size(TIME)
    lags = old_stack.shape[0]
    z, yh, zs = lax.axis_index("z"), lax.axis_index("yh"), lax.axis_size("z")
    reach = half_taps + PAD
    edge = facing_edge(raw_strain, reach)
    pairs = [(i, i + 1) for i in range(1, segments - 1, 2)]
    across = lax.ppermute(edge, TIME, pairs + [(b, a) for a, b in pairs])
    beside = turned(raw_strain, "c", 1)
    prepared = prepare(whitening, raw_strain)
    mine, own = filter_segment(beside, across, prepared, half_taps)
    other = turned(mine, "yh", 1)
    pieces = []
    for d in range(zs):
        piece = turned(own, "z", (zs - d) % zs) if d else own
        pieces.append(piece)
    mine_swapped = turned(mine, "c", 1)
    pieces += [mine_swapped, turned(jnp.concatenate(pieces[1:], axis=0), "c", 1)]
    lag_count = lags * segments // 2
    other_swapped = turned(other, "c", 1)
    mine_rows = lagged_rows(mine, mine_swapped, lag_count)
    other_rows = lagged_rows(other, other_swapped, lag_count)
    sums = {}
    for d in (2, 1, 3, 0):
        sums[d] = chunk(pieces, mine_rows, other_rows, d)
        if d:
            sums[d] = passed(sums[d], d, 0)
    own_part, *parts = middle(*[sums[d] for d in range(4)])
    parts = [own_part] + [passed(part, d, 1) for d, part in enumerate(parts, 1)]
    scaling = float(seg_len * segments) ** (-0.5)
    weights = jnp.repeat(block_mask[yh * zs + z].astype(jnp.float32) * scaling, channels)[None, :]
    return stack(parts, weights, old_stack)


def solution(mesh):
    fine = Mesh(mesh.devices.reshape(2, 4, 4, 2, 2), CHAN + TIME)
    in_specs = (P(CHAN, TIME), P(), P(), P(TIME, CHAN, None))
    out_specs = P(TIME, CHAN, None)
    return jax.shard_map(shards, mesh=fine, in_specs=in_specs, out_specs=out_specs, check_vma=False)
```

```python
import functools

import jax
import jax.numpy as jnp
from jax import lax
from jax.experimental import pallas as pl
from jax.experimental.pallas import tpu as pltpu
from jax.sharding import Mesh, PartitionSpec as P


CHAN = ("yh", "z")
TIME = ("x", "yl", "c")
VMEM = pl.BlockSpec(memory_space=pltpu.VMEM)
NT = (((1,), (1,)), ((), ()))
TILE = 256
PAD = 128
MIB = 1 << 20
SCALE = 4096.0


def call(kernel, out_shape, operands, mib, flops):
    return pl.pallas_call(
        kernel,
        out_shape=out_shape,
        in_specs=[VMEM] * len(operands),
        out_specs=jax.tree.map(lambda _: VMEM, out_shape),
        compiler_params=pltpu.CompilerParams(vmem_limit_bytes=mib * MIB),
        cost_estimate=pl.CostEstimate(flops=flops, bytes_accessed=MIB, transcendentals=0),
    )(*operands)


def split(value):
    high = value.astype(jnp.bfloat16)
    return high, (value - high.astype(jnp.float32)).astype(jnp.bfloat16)


def prepare_kernel(taps_ref, own_ref, high_ref, low_ref, own_high_ref, own_low_ref):
    own_high_ref[...], own_low_ref[...] = split(own_ref[...])
    rows, width = high_ref.shape
    taps = taps_ref[...]
    row = jnp.concatenate([taps, jnp.zeros((1, width - taps.shape[1]), jnp.float32)], axis=1)
    matrix = pltpu.roll(jnp.broadcast_to(row, (rows, width)), 0, 1, stride=1, stride_axis=0)
    high_ref[...], low_ref[...] = split(matrix)


def prepare(whitening, own):
    matrix = jax.ShapeDtypeStruct((TILE, whitening.shape[0] + TILE), jnp.bfloat16)
    part = jax.ShapeDtypeStruct(own.shape, jnp.bfloat16)
    shapes = (matrix, matrix, part, part)
    return call(prepare_kernel, shapes, (whitening[None, :], own), 8, 10**9)


def filter_kernel(
    half_taps, beside_ref, across_ref, mat_high_ref, mat_low_ref, own_high_ref, own_low_ref, mine_ref, own_ref
):
    channels, seg_len = own_ref.shape
    width = mat_high_ref.shape[1]
    blocks = seg_len // TILE + 1
    lower = lax.axis_index("c") == 0
    reach = half_taps + PAD
    across = across_ref[...]
    low = split(jnp.where(lower, across, beside_ref[:, seg_len - reach :]))
    high = split(jnp.where(lower, beside_ref[:, :half_taps], across[:, :half_taps]))

    def stacked(before, own, after):
        zeros = jnp.zeros((channels, TILE - PAD), jnp.bfloat16)
        padded = jnp.concatenate([zeros, before, own, after], axis=1)
        return jnp.concatenate(
            [padded[:, b * TILE : b * TILE + width] for b in range(blocks)], axis=0
        )

    x_high = stacked(low[0], own_high_ref[...], high[0])
    x_low = stacked(low[1], own_low_ref[...], high[1])
    dot = functools.partial(lax.dot_general, dimension_numbers=NT, preferred_element_type=jnp.float32)
    total = dot(x_low, mat_high_ref[...]) + dot(x_high, mat_low_ref[...])
    total = total + dot(x_high, mat_high_ref[...])
    before = total[:channels, TILE - PAD :]
    before = jnp.where(lax.axis_index(TIME) == 0, jnp.zeros_like(before), before)
    mine_ref[:, :PAD] = before.astype(jnp.bfloat16)
    for b in range(1, blocks):
        piece = total[b * channels : (b + 1) * channels].astype(jnp.bfloat16)
        mine_ref[:, PAD + (b - 1) * TILE : PAD + b * TILE] = piece
        own_ref[:, (b - 1) * TILE : b * TILE] = piece


def filter_segment(beside, across, prepared, half_taps):
    channels, seg_len = beside.shape
    return call(
        functools.partial(filter_kernel, half_taps),
        (
            jax.ShapeDtypeStruct((channels, PAD + seg_len), jnp.bfloat16),
            jax.ShapeDtypeStruct((channels, seg_len), jnp.bfloat16),
        ),
        (beside, across, *prepared),
        12,
        10**9,
    )


def rows_kernel(lag_count, segment_ref, rows_ref):
    channels = segment_ref.shape[0]
    core = lax.axis_index("c")
    segment = segment_ref[...]
    segment = jnp.where(core == 0, segment, pltpu.roll(segment, 2, 1))
    groups = lag_count // 2
    for index in range(lag_count):
        group, second = index // 2, index % 2
        lag = 4 * group + second
        moved = segment if lag == 0 else pltpu.roll(segment, lag, 1)
        place = jnp.where(core == 0, group, group % 2 * (groups // 2) + group // 2)
        at = pl.ds(pl.multiple_of((2 * place + second) * channels, channels), channels)
        rows_ref[at, :] = moved[:, PAD:]


def lagged_rows(segment, lag_count):
    channels, width = segment.shape
    shape = jax.ShapeDtypeStruct((lag_count * channels, width - PAD), jnp.bfloat16)
    return call(functools.partial(rows_kernel, lag_count), shape, (segment,), 4, 10**9)


def position():
    core, x, y = lax.axis_index("c"), lax.axis_index("x"), 2 * lax.axis_index("yh") + lax.axis_index("yl")
    return core, x, y


def chunk_kernel(distance, halves, *refs):
    *refs, out_ref = refs
    start_refs = [] if 0 in halves else [refs.pop()]
    row_refs = refs[-2 * len(halves) :]
    mine_ref, other_ref = row_refs[: len(halves)], row_refs[len(halves) :]
    col_refs = refs[: -2 * len(halves)]
    seg_len = col_refs[0].shape[1] if 0 in halves else col_refs[-1].shape[1]
    rows = out_ref.shape[0] // 2
    core, x, y = position()
    yh = lax.axis_index("yh")
    to_x, to_y = lax.rem(x + distance, 4), lax.rem(y + distance, 4)

    def fill(first_ref, second_ref, first_at, second_at):
        total = sum(ref[...] for ref in start_refs)
        for k, half in enumerate(halves):
            parts = col_refs[-2:] if half else col_refs[:4]
            cols = jnp.concatenate([ref[:, ref.shape[1] - seg_len :] for ref in parts], axis=0)
            left = jnp.concatenate(
                [
                    ref[k][pl.ds(pl.multiple_of(at, rows), rows), :]
                    for ref, at in ((first_ref, first_at), (second_ref, second_at))
                ],
                axis=0,
            )
            total = total + lax.dot_general(left, cols, NT, preferred_element_type=jnp.float32)
        out_ref[...] = total.astype(out_ref.dtype)

    along_x = to_x * rows
    along_y = lax.rem(to_y, 2) * 2 * rows
    stays = to_y // 2 == yh
    is_x = core == 0

    @pl.when(is_x & (yh == 0))
    def _():
        fill(mine_ref, other_ref, along_x, along_x)

    @pl.when(is_x & (yh != 0))
    def _():
        fill(other_ref, mine_ref, along_x, along_x)

    @pl.when(jnp.logical_not(is_x) & stays)
    def _():
        fill(mine_ref, mine_ref, along_y, along_y + rows)

    @pl.when(jnp.logical_not(is_x) & jnp.logical_not(stays))
    def _():
        fill(other_ref, other_ref, along_y, along_y + rows)


def chunk(pieces, rows, distance, halves=(0, 1), start=()):
    width = pieces[0].shape[0] * (len(pieces) - 2)
    whole = distance == 0 or 1 not in halves
    cols = (pieces[:-2] if 0 in halves else []) + (pieces[-2:] if 1 in halves else [])
    rows = [rows[2 * k + half] for k in range(2) for half in halves]
    return call(
        functools.partial(chunk_kernel, distance, halves),
        jax.ShapeDtypeStruct((rows[0].shape[0] // 2, width), jnp.float32 if whole else jnp.bfloat16),
        (*cols, *rows, *start),
        6,
        10**9,
    )


def by_column_half(own, first, second, third):
    last = lax.axis_index("yl") == 0
    near, far = jnp.where(last, third, first), jnp.where(last, first, third)
    return own + near, second + far


def middle_kernel(own_ref, first_ref, second_ref, third_ref, own_out_ref, *out_refs):
    rows = own_out_ref.shape[1]
    core, x, y = position()
    base = jnp.where(core == 0, y, x)
    for distance, out_ref in enumerate((own_out_ref, *out_refs)):
        at = pl.ds(pl.multiple_of(lax.rem(base + distance, 4) * rows, rows), rows)
        own = own_ref[at, :]
        parts = [ref[at, :].astype(jnp.float32) for ref in (first_ref, second_ref, third_ref)]
        total = own + parts[0] + parts[1] + parts[2]
        same, cross = by_column_half(own, *parts)
        if distance == 0:
            out_ref[0] = jnp.where(core == 0, total, same)
            out_ref[1] = jnp.where(core == 0, jnp.zeros_like(total), cross)
        else:
            rounded = total.astype(jnp.bfloat16).astype(jnp.float32)
            out_ref[0] = jnp.where(core == 0, rounded, same).astype(jnp.bfloat16)
            out_ref[1] = jnp.where(core == 0, total - rounded, cross).astype(jnp.bfloat16)


def middle(own, first, second, third):
    rows, width = own.shape
    shape = (2, rows // 4, width)
    shapes = (jax.ShapeDtypeStruct(shape, jnp.float32),) + (jax.ShapeDtypeStruct(shape, jnp.bfloat16),) * 3
    return call(middle_kernel, shapes, (own, first, second, third), 8, 10**9)


def stack_kernel(own_ref, first_ref, second_ref, third_ref, weights_ref, old_ref, out_ref):
    width = own_ref.shape[-1]
    core, _, _ = position()
    yh = lax.axis_index("yh")
    pairs = [[ref[h].astype(jnp.float32) for h in range(2)] for ref in (first_ref, second_ref, third_ref)]
    x_last = [own_ref[h] + pairs[0][h] + pairs[1][h] + pairs[2][h] for h in range(2)]
    y_last = by_column_half(own_ref[0], *[a + b for a, b in pairs])
    turn = lax.axis_index("z") * (out_ref.shape[0] // 2)
    for h in range(2):
        total = pltpu.roll(jnp.where(core == 0, y_last[h], x_last[h]), turn, 1)
        half = yh if h == 0 else 1 - yh
        at = pl.ds(pl.multiple_of(half * width, width), width)
        out_ref[:, at] = old_ref[:, at] + total * weights_ref[:, at]


def stack(parts, weights, old_stack):
    lags, channels, width = old_stack.shape
    shape = jax.ShapeDtypeStruct((lags * channels, width), jnp.float32)
    old = old_stack.reshape(lags * channels, width)
    return call(stack_kernel, shape, (*parts, weights, old), 8, 10**8).reshape(old_stack.shape)


def passed(value, distance, x_core):
    axes = ("yh", "x", "yl", "c")
    pairs = []
    for x in range(4):
        for y in range(4):
            for core in range(2):
                to_x, to_y = ((x + distance) % 4, y) if core == x_core else (x, (y + distance) % 4)
                source, target = (((b // 2 * 4 + a) * 2 + b % 2) * 2 + core for a, b in ((x, y), (to_x, to_y)))
                pairs.append((source, target))
    return lax.ppermute(value, axes, pairs)


def turned(value, axis, distance):
    size = lax.axis_size(axis)
    return lax.ppermute(value, axis, [(i, (i + distance) % size) for i in range(size)])


def shards(raw_strain, whitening, block_mask, old_stack):
    channels, seg_len = raw_strain.shape
    half_taps = whitening.shape[0] // 2
    segments = lax.axis_size(TIME)
    lags = old_stack.shape[0]
    core, z, yh, zs = lax.axis_index("c"), lax.axis_index("z"), lax.axis_index("yh"), lax.axis_size("z")
    reach = half_taps + PAD
    edge = jnp.where(core == 0, raw_strain[:, :reach], raw_strain[:, seg_len - reach :])
    edge = (edge * SCALE).astype(jnp.float16)
    pairs = [(i, i + 1) for i in range(1, segments - 1, 2)]
    across = lax.ppermute(edge, TIME, pairs + [(b, a) for a, b in pairs])
    across = across.astype(jnp.float32) * (1.0 / SCALE)
    beside = turned(raw_strain, "c", 1)
    prepared = prepare(whitening, raw_strain)
    mine, own = filter_segment(beside, across, prepared, half_taps)
    other = turned(mine, "yh", 1)
    pieces = []
    for d in range(zs):
        piece = turned(own, "z", (zs - d) % zs) if d else own
        pieces.append(piece)
    mine_swapped = turned(mine, "c", 1)
    pieces += [mine_swapped, turned(jnp.concatenate(pieces[1:], axis=0), "c", 1)]
    lag_count = lags * segments // 2
    other_swapped = turned(other, "c", 1)
    sources = (mine, mine_swapped, other, other_swapped)
    rows = [lagged_rows(segment, lag_count) for segment in sources]
    sums = {}
    lead = chunk(pieces, rows, 1, (0,))
    for d in (1, 3, 2, 0):
        sums[d] = chunk(pieces, rows, d, (1,), (lead,)) if d == 1 else chunk(pieces, rows, d)
        if d:
            sums[d] = passed(sums[d], d, 0)
    own_part, *parts = middle(*[sums[d] for d in range(4)])
    parts = [own_part] + [passed(part, d, 1) for d, part in enumerate(parts, 1)]
    scaling = float(seg_len * segments) ** (-0.5)
    weights = jnp.repeat(block_mask[yh * zs + z].astype(jnp.float32) * scaling, channels)[None, :]
    return stack(parts, weights, old_stack)


def solution(mesh):
    fine = Mesh(mesh.devices.reshape(2, 4, 4, 2, 2), CHAN + TIME)
    in_specs = (P(CHAN, TIME), P(), P(), P(TIME, CHAN, None))
    out_specs = P(TIME, CHAN, None)
    return jax.shard_map(shards, mesh=fine, in_specs=in_specs, out_specs=out_specs, check_vma=False)
```

```python
import functools

import jax
import jax.numpy as jnp
from jax import lax
from jax.experimental import pallas as pl
from jax.experimental.pallas import tpu as pltpu
from jax.sharding import Mesh, PartitionSpec as P


CHAN = ("yh", "z")
TIME = ("x", "yl", "c")
VMEM = pl.BlockSpec(memory_space=pltpu.VMEM)
NT = (((1,), (1,)), ((), ()))
TILE = 256
PAD = 128
MIB = 1 << 20
SCALE = 4096.0


def call(kernel, out_shape, operands, mib, flops):
    return pl.pallas_call(
        kernel,
        out_shape=out_shape,
        in_specs=[VMEM] * len(operands),
        out_specs=jax.tree.map(lambda _: VMEM, out_shape),
        compiler_params=pltpu.CompilerParams(vmem_limit_bytes=mib * MIB),
        cost_estimate=pl.CostEstimate(flops=flops, bytes_accessed=MIB, transcendentals=0),
    )(*operands)


def split(value):
    high = value.astype(jnp.bfloat16)
    return high, (value - high.astype(jnp.float32)).astype(jnp.bfloat16)


def prepare_kernel(taps_ref, own_ref, high_ref, low_ref, own_high_ref, own_low_ref):
    own_high_ref[...], own_low_ref[...] = split(own_ref[...])
    rows, width = high_ref.shape
    taps = taps_ref[...]
    row = jnp.concatenate([taps, jnp.zeros((1, width - taps.shape[1]), jnp.float32)], axis=1)
    matrix = pltpu.roll(jnp.broadcast_to(row, (rows, width)), 0, 1, stride=1, stride_axis=0)
    high_ref[...], low_ref[...] = split(matrix)


def prepare(whitening, own):
    matrix = jax.ShapeDtypeStruct((TILE, whitening.shape[0] + TILE), jnp.bfloat16)
    part = jax.ShapeDtypeStruct(own.shape, jnp.bfloat16)
    shapes = (matrix, matrix, part, part)
    return call(prepare_kernel, shapes, (whitening[None, :], own), 8, 10**9)


def filter_kernel(
    half_taps, beside_ref, across_ref, mat_high_ref, mat_low_ref, own_high_ref, own_low_ref, mine_ref, own_ref
):
    channels, seg_len = own_ref.shape
    width = mat_high_ref.shape[1]
    blocks = seg_len // TILE + 1
    lower = lax.axis_index("c") == 0
    reach = half_taps + PAD
    across = across_ref[...]
    low = split(jnp.where(lower, across, beside_ref[:, seg_len - reach :]))
    high = split(jnp.where(lower, beside_ref[:, :half_taps], across[:, :half_taps]))

    def stacked(before, own, after):
        zeros = jnp.zeros((channels, TILE - PAD), jnp.bfloat16)
        padded = jnp.concatenate([zeros, before, own, after], axis=1)
        return jnp.concatenate(
            [padded[:, b * TILE : b * TILE + width] for b in range(blocks)], axis=0
        )

    x_high = stacked(low[0], own_high_ref[...], high[0])
    x_low = stacked(low[1], own_low_ref[...], high[1])
    dot = functools.partial(lax.dot_general, dimension_numbers=NT, preferred_element_type=jnp.float32)
    total = dot(x_low, mat_high_ref[...]) + dot(x_high, mat_low_ref[...])
    total = total + dot(x_high, mat_high_ref[...])
    before = total[:channels, TILE - PAD :]
    before = jnp.where(lax.axis_index(TIME) == 0, jnp.zeros_like(before), before)
    mine_ref[:, :PAD] = before.astype(jnp.bfloat16)
    for b in range(1, blocks):
        piece = total[b * channels : (b + 1) * channels].astype(jnp.bfloat16)
        mine_ref[:, PAD + (b - 1) * TILE : PAD + b * TILE] = piece
        own_ref[:, (b - 1) * TILE : b * TILE] = piece


def filter_segment(beside, across, prepared, half_taps):
    channels, seg_len = beside.shape
    return call(
        functools.partial(filter_kernel, half_taps),
        (
            jax.ShapeDtypeStruct((channels, PAD + seg_len), jnp.bfloat16),
            jax.ShapeDtypeStruct((channels, seg_len), jnp.bfloat16),
        ),
        (beside, across, *prepared),
        12,
        10**9,
    )


def rows_kernel(lag_count, segment_ref, rows_ref):
    channels = segment_ref.shape[0]
    groups = lag_count // 2

    def fill(core):
        for index in range(lag_count):
            group, second = index // 2, index % 2
            lag = 4 * group + second + 2 * core
            place = group % 2 * (groups // 2) + group // 2 if core else group
            at = (2 * place + second) * channels
            for k in range(0, channels, 16):
                strip = segment_ref[k : k + 16, :]
                moved = pltpu.roll(strip, lag, 1) if lag else strip
                rows_ref[at + k : at + k + 16, :] = moved[:, PAD:]

    pl.when(lax.axis_index("c") == 0)(lambda: fill(0))
    pl.when(lax.axis_index("c") != 0)(lambda: fill(1))


def lagged_rows(segment, lag_count):
    channels, width = segment.shape
    shape = jax.ShapeDtypeStruct((lag_count * channels, width - PAD), jnp.bfloat16)
    return call(functools.partial(rows_kernel, lag_count), shape, (segment,), 4, 10**9)


def position():
    core, x, y = lax.axis_index("c"), lax.axis_index("x"), 2 * lax.axis_index("yh") + lax.axis_index("yl")
    return core, x, y


def chunk_kernel(distance, halves, *refs):
    *refs, out_ref = refs
    start_refs = [] if 0 in halves else [refs.pop()]
    row_refs = refs[-2 * len(halves) :]
    mine_ref, other_ref = row_refs[: len(halves)], row_refs[len(halves) :]
    col_refs = refs[: -2 * len(halves)]
    seg_len = col_refs[0].shape[1] if 0 in halves else col_refs[-1].shape[1]
    rows = out_ref.shape[0] // 2
    core, x, y = position()
    yh = lax.axis_index("yh")
    to_x, to_y = lax.rem(x + distance, 4), lax.rem(y + distance, 4)

    def fill(first_ref, second_ref, first_at, second_at):
        total = sum(ref[...] for ref in start_refs)
        for k, half in enumerate(halves):
            parts = col_refs[-2:] if half else col_refs[:4]
            cols = jnp.concatenate([ref[:, ref.shape[1] - seg_len :] for ref in parts], axis=0)
            left = jnp.concatenate(
                [
                    ref[k][pl.ds(pl.multiple_of(at, rows), rows), :]
                    for ref, at in ((first_ref, first_at), (second_ref, second_at))
                ],
                axis=0,
            )
            total = total + lax.dot_general(left, cols, NT, preferred_element_type=jnp.float32)
        out_ref[...] = total.astype(out_ref.dtype)

    along_x = to_x * rows
    along_y = lax.rem(to_y, 2) * 2 * rows
    stays = to_y // 2 == yh
    is_x = core == 0

    @pl.when(is_x & (yh == 0))
    def _():
        fill(mine_ref, other_ref, along_x, along_x)

    @pl.when(is_x & (yh != 0))
    def _():
        fill(other_ref, mine_ref, along_x, along_x)

    @pl.when(jnp.logical_not(is_x) & stays)
    def _():
        fill(mine_ref, mine_ref, along_y, along_y + rows)

    @pl.when(jnp.logical_not(is_x) & jnp.logical_not(stays))
    def _():
        fill(other_ref, other_ref, along_y, along_y + rows)


def chunk(pieces, rows, distance, halves=(0, 1), start=()):
    width = pieces[0].shape[0] * (len(pieces) - 2)
    whole = distance == 0 or 1 not in halves
    cols = (pieces[:-2] if 0 in halves else []) + (pieces[-2:] if 1 in halves else [])
    rows = [rows[2 * k + half] for k in range(2) for half in halves]
    return call(
        functools.partial(chunk_kernel, distance, halves),
        jax.ShapeDtypeStruct((rows[0].shape[0] // 2, width), jnp.float32 if whole else jnp.bfloat16),
        (*cols, *rows, *start),
        6,
        10**9,
    )


def by_column_half(own, first, second, third):
    last = lax.axis_index("yl") == 0
    near, far = jnp.where(last, third, first), jnp.where(last, first, third)
    return own + near, second + far


def middle_kernel(own_ref, first_ref, second_ref, third_ref, own_out_ref, *out_refs):
    rows = own_out_ref.shape[1]
    core, x, y = position()
    base = jnp.where(core == 0, y, x)
    for distance, out_ref in enumerate((own_out_ref, *out_refs)):
        at = pl.ds(pl.multiple_of(lax.rem(base + distance, 4) * rows, rows), rows)
        own = own_ref[at, :]
        parts = [ref[at, :].astype(jnp.float32) for ref in (first_ref, second_ref, third_ref)]
        total = own + parts[0] + parts[1] + parts[2]
        same, cross = by_column_half(own, *parts)
        if distance == 0:
            out_ref[0] = jnp.where(core == 0, total, same)
            out_ref[1] = jnp.where(core == 0, jnp.zeros_like(total), cross)
        else:
            rounded = total.astype(jnp.bfloat16).astype(jnp.float32)
            out_ref[0] = jnp.where(core == 0, rounded, same).astype(jnp.bfloat16)
            out_ref[1] = jnp.where(core == 0, total - rounded, cross).astype(jnp.bfloat16)


def middle(own, first, second, third):
    rows, width = own.shape
    shape = (2, rows // 4, width)
    shapes = (jax.ShapeDtypeStruct(shape, jnp.float32),) + (jax.ShapeDtypeStruct(shape, jnp.bfloat16),) * 3
    return call(middle_kernel, shapes, (own, first, second, third), 8, 10**9)


def stack_kernel(own_ref, first_ref, second_ref, third_ref, weights_ref, old_ref, out_ref):
    width = own_ref.shape[-1]
    core, _, _ = position()
    yh = lax.axis_index("yh")
    pairs = [[ref[h].astype(jnp.float32) for h in range(2)] for ref in (first_ref, second_ref, third_ref)]
    x_last = [own_ref[h] + pairs[0][h] + pairs[1][h] + pairs[2][h] for h in range(2)]
    y_last = by_column_half(own_ref[0], *[a + b for a, b in pairs])
    turn = lax.axis_index("z") * (out_ref.shape[0] // 2)
    for h in range(2):
        total = pltpu.roll(jnp.where(core == 0, y_last[h], x_last[h]), turn, 1)
        half = yh if h == 0 else 1 - yh
        at = pl.ds(pl.multiple_of(half * width, width), width)
        out_ref[:, at] = old_ref[:, at] + total * weights_ref[:, at]


def stack(parts, weights, old_stack):
    lags, channels, width = old_stack.shape
    shape = jax.ShapeDtypeStruct((lags * channels, width), jnp.float32)
    old = old_stack.reshape(lags * channels, width)
    return call(stack_kernel, shape, (*parts, weights, old), 8, 10**8).reshape(old_stack.shape)


def passed(value, distance, x_core):
    axes = ("yh", "x", "yl", "c")
    pairs = []
    for x in range(4):
        for y in range(4):
            for core in range(2):
                to_x, to_y = ((x + distance) % 4, y) if core == x_core else (x, (y + distance) % 4)
                source, target = (((b // 2 * 4 + a) * 2 + b % 2) * 2 + core for a, b in ((x, y), (to_x, to_y)))
                pairs.append((source, target))
    return lax.ppermute(value, axes, pairs)


def turned(value, axis, distance):
    size = lax.axis_size(axis)
    return lax.ppermute(value, axis, [(i, (i + distance) % size) for i in range(size)])


def shards(raw_strain, whitening, block_mask, old_stack):
    channels, seg_len = raw_strain.shape
    half_taps = whitening.shape[0] // 2
    segments = lax.axis_size(TIME)
    lags = old_stack.shape[0]
    core, z, yh, zs = lax.axis_index("c"), lax.axis_index("z"), lax.axis_index("yh"), lax.axis_size("z")
    reach = half_taps + PAD
    edge = lax.dynamic_slice_in_dim(raw_strain, core * (seg_len - reach), reach, 1)
    edge = (edge * SCALE).astype(jnp.float16)
    pairs = [(i, i + 1) for i in range(1, segments - 1, 2)]
    across = lax.ppermute(edge, TIME, pairs + [(b, a) for a, b in pairs])
    across = across.astype(jnp.float32) * (1.0 / SCALE)
    beside = turned(raw_strain, "c", 1)
    prepared = prepare(whitening, raw_strain)
    mine, own = filter_segment(beside, across, prepared, half_taps)
    other = turned(mine, "yh", 1)
    pieces = []
    for d in range(zs):
        piece = turned(own, "z", (zs - d) % zs) if d else own
        pieces.append(piece)
    mine_swapped = turned(mine, "c", 1)
    pieces += [mine_swapped, turned(jnp.concatenate(pieces[1:], axis=0), "c", 1)]
    lag_count = lags * segments // 2
    other_swapped = turned(other, "c", 1)
    sources = (mine, mine_swapped, other, other_swapped)
    rows = [lagged_rows(segment, lag_count) for segment in sources]
    sums = {}
    lead = chunk(pieces, rows, 1, (0,))
    for d in (1, 3, 2, 0):
        sums[d] = chunk(pieces, rows, d, (1,), (lead,)) if d == 1 else chunk(pieces, rows, d)
        if d:
            sums[d] = passed(sums[d], d, 0)
    own_part, *parts = middle(*[sums[d] for d in range(4)])
    parts = [own_part] + [passed(part, d, 1) for d, part in enumerate(parts, 1)]
    scaling = float(seg_len * segments) ** (-0.5)
    weights = jnp.repeat(block_mask[yh * zs + z].astype(jnp.float32) * scaling, channels)[None, :]
    return stack(parts, weights, old_stack)


def solution(mesh):
    fine = Mesh(mesh.devices.reshape(2, 4, 4, 2, 2), CHAN + TIME)
    in_specs = (P(CHAN, TIME), P(), P(), P(TIME, CHAN, None))
    out_specs = P(TIME, CHAN, None)
    return jax.shard_map(shards, mesh=fine, in_specs=in_specs, out_specs=out_specs, check_vma=False)
```
